32 devices in a mesh: section: 2 (over y), ctx: 4 (over x, core), tensor: 4 (over z).
Axes of the slice: x: 2, y: 2, z: 4, core: 2. Of those that a mesh axis runs over, the one named last changes fastest.
Arguments:
- block_input: bfloat16 [2, 1, 704, 1024], P(None, None, 'ctx'), may hold values from -6 to 6
- cotangent: bfloat16 [2, 1, 704, 1024], P(None, None, 'ctx'), may hold values from -6 to 6
- lengths: int32 [2, 1], replicated, may hold values from 352 to 704, as said below
- projection: bfloat16 [2, 3, 1024, 1024], P('section', None, 'ctx', 'tensor')
- projectionbias: bfloat16 [2, 2, 16, 64], P('section', None, 'tensor', 'ctx'), may hold values from -3 to 3
- merger: bfloat16 [2, 1024, 1024], P('section', 'tensor', 'ctx'), may hold values from -0.75 to 0.75
- mergerbias: bfloat16 [2, 1024], P('section', 'ctx'), may hold values from -2 to 2
- expander: bfloat16 [2, 1024, 4096], P('section', 'ctx', 'tensor'), may hold values from -0.1875 to 0.1875
- expanderbias: bfloat16 [2, 4, 1024], P('section', 'tensor', 'ctx'), may hold values from -3 to 3
- reducer: bfloat16 [2, 4096, 1024], P('section', 'tensor', 'ctx'), may hold values from -0.09375 to 0.09375
- reducerbias: bfloat16 [2, 1024], P('section', 'ctx'), may hold values from -2 to 2
- firstgain: bfloat16 [2, 1024], P('section', 'ctx'), may hold values from 0.25 to 1.75
- firstshift: bfloat16 [2, 1024], P('section', 'ctx'), may hold values from -2 to 2
- secondgain: bfloat16 [2, 1024], P('section', 'ctx'), may hold values from 0.25 to 1.75
- secondshift: bfloat16 [2, 1024], P('section', 'ctx'), may hold values from -2 to 2
- attentionscale: bfloat16 [2, 1024], P('section', 'ctx'), may hold values from 0.3984375 to 2
- feedforwardscale: bfloat16 [2, 1024], P('section', 'ctx'), may hold values from 0.3984375 to 2
Outputs:
- block_output: bfloat16 [2, 1, 704, 1024], P(None, None, 'ctx', 'section')
- input_grad: float32 [2, 1, 704, 1024], P(None, None, 'ctx', 'section')
- grad_projection: float32 [2, 3, 1024, 1024], P('section', None, 'ctx', 'tensor')
- grad_projectionbias: float32 [2, 2, 16, 64], P('section', None, 'tensor', 'ctx')
- grad_merger: float32 [2, 1024, 1024], P('section', 'tensor', 'ctx')
- grad_mergerbias: float32 [2, 1024], P('section', 'ctx')
- grad_expander: float32 [2, 1024, 4096], P('section', 'ctx', 'tensor')
- grad_expanderbias: float32 [2, 4, 1024], P('section', 'tensor', 'ctx')
- grad_reducer: float32 [2, 4096, 1024], P('section', 'tensor', 'ctx')
- grad_reducerbias: float32 [2, 1024], P('section', 'ctx')
- grad_firstgain: float32 [2, 1024], P('section', 'ctx')
- grad_firstshift: float32 [2, 1024], P('section', 'ctx')
- grad_secondgain: float32 [2, 1024], P('section', 'ctx')
- grad_secondshift: float32 [2, 1024], P('section', 'ctx')
- grad_attentionscale: float32 [2, 1024], P('section', 'ctx')
- grad_feedforwardscale: float32 [2, 1024], P('section', 'ctx')
The draws below stay inside these ranges and needn't reach their ends.
Inputs may be any that keep to these rules, and one draw needn't show every extreme that they name: `lengths`: valid tokens of each image; positions from it on are padding; some image is full.
All inputs are finite; a program needn't handle non-finite values.
Results may differ from the reference program's by a relative error of at most 0.025.
Values may be sent and summed in bfloat16 or wider, within the bound.
A program may use at most 128 MiB of HBM per device.

```python
import math
import jax
import jax.numpy as jnp
from jax import lax

D = 1024
HEADS = 16
HD = 64
FF = 4096
IMG = 1
MB = 2
SEQ = 704
LAYERS = 2
FF_DEV = 1024
N_TENSOR = 4


def draw_projection(key, part):
    base = jax.random.normal(jax.random.fold_in(key, 11), (LAYERS, 3, D, D), jnp.float32) * D ** (-0.5)
    return base.astype(jnp.bfloat16)


def draw_lengths(key, part):
    drawn = jax.random.randint(jax.random.fold_in(key, 21), (MB * IMG,), SEQ // 2, SEQ + 1, dtype=jnp.int32)
    chosen = jax.random.randint(jax.random.fold_in(key, 22), (), 0, MB * IMG, dtype=jnp.int32)
    filled = jnp.where(jnp.arange(MB * IMG, dtype=jnp.int32) == chosen, SEQ, drawn)
    return filled.reshape(MB, IMG).astype(jnp.int32)


def block_levels(stream_key, shape, pieces, least, top_value):
    def one(axis_at, blocks):
        steps = jax.random.uniform(jax.random.fold_in(jax.random.fold_in(stream_key, 6), axis_at), (blocks,), jnp.float32, least / len(pieces), top_value / len(pieces))
        return jnp.repeat(jnp.exp(steps), shape[axis_at] // blocks).reshape((-1,) + (1,) * (len(shape) - axis_at - 1))

    level = one(*pieces[0])
    for cut in pieces[1:]:
        level = level * one(*cut)
    return level


def normal_values(stream_key, dims, scale, bound, split=(), kind=jnp.bfloat16):
    level = block_levels(stream_key, dims, split, -0.22, 0.18) if split else 1.0
    result = jax.random.normal(stream_key, dims, jnp.float32) * scale * level
    return jnp.minimum(jnp.maximum(result, -bound), bound).astype(kind)


def setup_inputs(seed: int = 0) -> dict:
    streams_of = jax.random.split(jax.random.key(seed), 18)
    return {
        "block_input": normal_values(streams_of[0], (MB, IMG, SEQ, D), 1.0, 6.0, ((2, 4),)),
        "cotangent": normal_values(streams_of[1], (MB, IMG, SEQ, D), 1.0, 6.0, ((2, 4),)),
        "lengths": draw_lengths(jax.random.fold_in(streams_of[17], 71), 0),
        "projection": draw_projection(jax.random.fold_in(streams_of[17], 71), 0),
        "projectionbias": normal_values(streams_of[4], (LAYERS, 2, HEADS, HD), 0.5, 3.0, ((0, 2), (2, 4), (3, 4))),
        "merger": normal_values(streams_of[5], (LAYERS, D, D), (D // 16) ** -0.5, 0.75, ((0, 2), (1, 4), (2, 4))),
        "mergerbias": normal_values(streams_of[6], (LAYERS, D), 0.3, 2.0, ((0, 2), (1, 4))),
        "expander": normal_values(streams_of[7], (LAYERS, D, FF), D ** -0.5, 0.1875, ((0, 2), (1, 4), (2, 4))),
        "expanderbias": normal_values(streams_of[8], (LAYERS, N_TENSOR, FF_DEV), 0.5, 3.0, ((0, 2), (1, 4), (2, 4))),
        "reducer": normal_values(streams_of[9], (LAYERS, FF, D), FF ** -0.5, 0.09375, ((0, 2), (1, 4), (2, 4))),
        "reducerbias": normal_values(streams_of[10], (LAYERS, D), 0.3, 2.0, ((0, 2), (1, 4))),
        "firstgain": jnp.clip(1.0 + 0.15 * jax.random.normal(streams_of[11], (LAYERS, D), jnp.float32), 0.25, 1.75).astype(jnp.bfloat16),
        "firstshift": normal_values(streams_of[12], (LAYERS, D), 0.3, 2.0, ((0, 2), (1, 4))),
        "secondgain": jnp.clip(1.0 + 0.15 * jax.random.normal(streams_of[13], (LAYERS, D), jnp.float32), 0.25, 1.75).astype(jnp.bfloat16),
        "secondshift": normal_values(streams_of[14], (LAYERS, D), 0.3, 2.0, ((0, 2), (1, 4))),
        "attentionscale": jnp.clip(jnp.exp(math.log(2.0) - 1.6133518 * jax.random.uniform(streams_of[15], (LAYERS, D), jnp.float32) ** block_levels(streams_of[15], (LAYERS, D), ((0, 2), (1, 4)), -0.2, 0.2)), 0.3984375, 2.0).astype(jnp.bfloat16),
        "feedforwardscale": jnp.clip(jnp.exp(math.log(2.0) - 1.6133518 * jax.random.uniform(streams_of[16], (LAYERS, D), jnp.float32) ** block_levels(streams_of[16], (LAYERS, D), ((0, 2), (1, 4)), -0.2, 0.2)), 0.3984375, 2.0).astype(jnp.bfloat16),
    }


EPSILON = 1e-06

def layer_norm(hidden, gain, shift):
    center = hidden - lax.optimization_barrier(jnp.mean(hidden, axis=-1, keepdims=True))
    inverse = lax.rsqrt(lax.optimization_barrier(jnp.mean(center * center, axis=-1, keepdims=True)) + EPSILON)
    normed = center * inverse
    return (normed, inverse, normed * gain + shift)

def norm_back(upstream, normed, inverse, gain):
    scaled = upstream * gain
    return inverse * (scaled - lax.optimization_barrier(jnp.mean(scaled, axis=-1, keepdims=True)) - normed * lax.optimization_barrier(jnp.mean(scaled * normed, axis=-1, keepdims=True)))

def gelu_slope(pre):
    cumulative = 0.5 * (1.0 + jax.scipy.special.erf(pre * 0.7071067811865476))
    return cumulative + pre * jnp.exp(-0.5 * pre * pre) * 0.3989422804014327

def group_sum(partials):
    return lax.optimization_barrier(jnp.sum(lax.optimization_barrier(partials.astype(jnp.bfloat16)).astype(jnp.float32), axis=0))

def split_product(left, right):
    tokens, inner = left.shape
    groups = left.reshape(tokens, N_TENSOR, inner // N_TENSOR).astype(jnp.float32)
    blocks = right.reshape(N_TENSOR, inner // N_TENSOR, right.shape[1]).astype(jnp.float32)
    return group_sum(jnp.einsum('ltc,tcd->tld', groups, blocks))

def head_view(rows):
    return rows.reshape(rows.shape[0], HEADS, HD).astype(jnp.float32)

def masked_scores(queries, key_rows, length):
    span = queries.shape[0]
    scores = jnp.einsum('qhd,khd->hqk', head_view(queries), head_view(key_rows)) * (1.0 / math.sqrt(HD))
    valid = jnp.arange(span, dtype=jnp.int32) < length
    return jnp.where(valid[None, None, :], scores, -jnp.inf)

def layer_forward(hidden, length, params):
    span = hidden.shape[0]
    normed_one, inverse_one, pre_one = layer_norm(hidden, params['first_gain'], params['first_shift'])
    normed_in = pre_one.astype(jnp.bfloat16)
    triple = jnp.einsum('ld,kde->kle', normed_in.astype(jnp.float32), params['projection'].astype(jnp.float32))
    queries = (triple[0] + params['query_bias']).astype(jnp.bfloat16)
    key_rows = triple[1].astype(jnp.bfloat16)
    value_rows = (triple[2] + params['value_bias']).astype(jnp.bfloat16)
    scores = masked_scores(queries, key_rows, length)
    largest = lax.optimization_barrier(jnp.max(scores, axis=-1, keepdims=True))
    expo = jnp.exp(scores - largest)
    total = lax.optimization_barrier(jnp.sum(expo, axis=-1, keepdims=True))
    weights = (expo / total).astype(jnp.bfloat16)
    mixed = jnp.einsum('hqk,khd->qhd', weights.astype(jnp.float32), head_view(value_rows))
    mixed = mixed.reshape(span, D).astype(jnp.bfloat16)
    log_total = largest + jnp.log(total)
    attn_out = split_product(mixed, params['merger']) + params['merger_bias']
    middle = hidden + params['attention_scale'] * attn_out
    normed_two, inverse_two, pre_two = layer_norm(middle, params['second_gain'], params['second_shift'])
    normed_mid = pre_two.astype(jnp.bfloat16)
    expanded = jnp.dot(normed_mid, params['expander'], preferred_element_type=jnp.float32) + params['expander_bias']
    activated = jax.nn.gelu(expanded, approximate=False).astype(jnp.bfloat16)
    reduced = split_product(activated, params['reducer']) + params['reducer_bias']
    output = middle + params['feedforward_scale'] * reduced
    saved = (normed_one, inverse_one, normed_in, queries, key_rows, value_rows, mixed, log_total, attn_out, normed_two, inverse_two, normed_mid, expanded, activated, reduced)
    return (output, saved)

def layer_backward(saved, upstream, length, params):
    normed_one, inverse_one, normed_in, queries, key_rows, value_rows, mixed, log_total, attn_out, normed_two, inverse_two, normed_mid, expanded, activated, reduced = saved
    span = upstream.shape[0]
    grad_fscale = lax.optimization_barrier(jnp.sum(upstream * reduced, axis=0))
    grad_reduced = upstream * params['feedforward_scale']
    grad_rbias = lax.optimization_barrier(jnp.sum(grad_reduced, axis=0))
    reduced_low = grad_reduced.astype(jnp.bfloat16)
    grad_reducer = jnp.dot(activated.T, reduced_low, preferred_element_type=jnp.float32)
    grad_act = jnp.dot(reduced_low, params['reducer'].T, preferred_element_type=jnp.float32)
    grad_pre = grad_act * gelu_slope(expanded)
    grad_ebias = lax.optimization_barrier(jnp.sum(grad_pre, axis=0))
    pre_low = grad_pre.astype(jnp.bfloat16)
    grad_expander = jnp.dot(normed_mid.T, pre_low, preferred_element_type=jnp.float32)
    grad_normed2 = split_product(pre_low, params['expander'].T)
    grad_sgain = lax.optimization_barrier(jnp.sum(grad_normed2 * normed_two, axis=0))
    grad_sshift = lax.optimization_barrier(jnp.sum(grad_normed2, axis=0))
    grad_middle = upstream + norm_back(grad_normed2, normed_two, inverse_two, params['second_gain'])
    grad_ascale = lax.optimization_barrier(jnp.sum(grad_middle * attn_out, axis=0))
    grad_attn = grad_middle * params['attention_scale']
    grad_mbias = lax.optimization_barrier(jnp.sum(grad_attn, axis=0))
    attn_low = grad_attn.astype(jnp.bfloat16)
    grad_merger = jnp.dot(mixed.T, attn_low, preferred_element_type=jnp.float32)
    grad_mixed = jnp.dot(attn_low, params['merger'].T, preferred_element_type=jnp.float32).astype(jnp.bfloat16)
    probs = jnp.exp(masked_scores(queries, key_rows, length) - log_total)
    probs_low = probs.astype(jnp.bfloat16)
    grad_heads = head_view(grad_mixed)
    grad_probs = jnp.einsum('qhd,khd->hqk', grad_heads, head_view(value_rows))
    inner = lax.optimization_barrier(jnp.sum(grad_heads * head_view(mixed), axis=-1))
    inner = jnp.transpose(inner, (1, 0))[..., None]
    grad_scores = (probs * (grad_probs - inner) * (1.0 / math.sqrt(HD))).astype(jnp.bfloat16)
    grad_queries = jnp.einsum('hqk,khd->qhd', grad_scores.astype(jnp.float32), head_view(key_rows)).reshape(span, D)
    grad_keys = jnp.einsum('hqk,qhd->khd', grad_scores.astype(jnp.float32), head_view(queries)).reshape(span, D)
    grad_values = jnp.einsum('hqk,qhd->khd', probs_low.astype(jnp.float32), grad_heads).reshape(span, D)
    grad_qvbias = jnp.stack([lax.optimization_barrier(jnp.sum(grad_queries, axis=0)), lax.optimization_barrier(jnp.sum(grad_values, axis=0))])
    stacked = jnp.stack([grad_queries, grad_keys, grad_values]).astype(jnp.bfloat16)
    grad_projection = jnp.einsum('ld,kle->kde', normed_in.astype(jnp.float32), stacked.astype(jnp.float32))
    groups = stacked.reshape(3, span, N_TENSOR, D // N_TENSOR).astype(jnp.float32)
    blocks = params['projection'].reshape(3, D, N_TENSOR, D // N_TENSOR).astype(jnp.float32)
    grad_normed1 = group_sum(jnp.einsum('klte,kdte->tld', groups, blocks))
    grad_fgain = lax.optimization_barrier(jnp.sum(grad_normed1 * normed_one, axis=0))
    grad_fshift = lax.optimization_barrier(jnp.sum(grad_normed1, axis=0))
    grad_input = grad_middle + norm_back(grad_normed1, normed_one, inverse_one, params['first_gain'])
    grads = (grad_projection, grad_qvbias, grad_merger, grad_mbias, grad_expander, grad_ebias, grad_reducer, grad_rbias, grad_fgain, grad_fshift, grad_sgain, grad_sshift, grad_ascale, grad_fscale)
    return (grad_input, grads)

def layer_params(weights, index):
    projection, projectionbias, merger, mergerbias, expander, expanderbias, reducer, reducerbias, firstgain, firstshift, secondgain, secondshift, attentionscale, feedforwardscale = weights
    return {'projection': projection[index], 'query_bias': projectionbias[index, 0].astype(jnp.float32).reshape(D), 'value_bias': projectionbias[index, 1].astype(jnp.float32).reshape(D), 'merger': merger[index], 'merger_bias': mergerbias[index].astype(jnp.float32), 'expander': expander[index], 'expander_bias': expanderbias[index].astype(jnp.float32).reshape(FF), 'reducer': reducer[index], 'reducer_bias': reducerbias[index].astype(jnp.float32), 'first_gain': firstgain[index].astype(jnp.float32), 'first_shift': firstshift[index].astype(jnp.float32), 'second_gain': secondgain[index].astype(jnp.float32), 'second_shift': secondshift[index].astype(jnp.float32), 'attention_scale': attentionscale[index].astype(jnp.float32), 'feedforward_scale': feedforwardscale[index].astype(jnp.float32)}

def reference(block_input, cotangent, lengths, projection, projectionbias, merger, mergerbias, expander, expanderbias, reducer, reducerbias, firstgain, firstshift, secondgain, secondshift, attentionscale, feedforwardscale):
    weights = (projection, projectionbias, merger, mergerbias, expander, expanderbias, reducer, reducerbias, firstgain, firstshift, secondgain, secondshift, attentionscale, feedforwardscale)
    first_params = layer_params(weights, 0)
    second_params = layer_params(weights, 1)
    grad_shapes = [(3, D, D), (2, D), (D, D), (D,), (D, FF), (FF,), (FF, D), (D,), (D,), (D,), (D,), (D,), (D,), (D,)]
    initial = tuple((jnp.zeros((LAYERS,) + shape, jnp.float32) for shape in grad_shapes))
    images = block_input.reshape(MB * IMG, SEQ, D)
    upstreams = cotangent.reshape(MB * IMG, SEQ, D)
    flat_lengths = lengths.reshape(MB * IMG).astype(jnp.int32)

    def image_step(carry, item):
        image, upstream, length = item
        first_out, first_saved = layer_forward(image.astype(jnp.float32), length, first_params)
        between = lax.optimization_barrier(first_out.astype(jnp.bfloat16)).astype(jnp.float32)
        second_out, second_saved = layer_forward(between, length, second_params)
        second_grad, second_grads = layer_backward(second_saved, upstream.astype(jnp.float32), length, second_params)
        first_grad, first_grads = layer_backward(first_saved, second_grad, length, first_params)
        carry = tuple((total + jnp.stack([lower, upper]) for total, lower, upper in zip(carry, first_grads, second_grads)))
        return (carry, (second_out.astype(jnp.bfloat16), first_grad))
    totals, (finals, input_grads) = lax.scan(image_step, initial, (images, upstreams, flat_lengths))
    return (finals.reshape(MB, IMG, SEQ, D), input_grads.reshape(MB, IMG, SEQ, D), totals[0], totals[1].reshape(LAYERS, 2, HEADS, HD), totals[2], totals[3], totals[4], totals[5].reshape(LAYERS, N_TENSOR, FF // N_TENSOR), totals[6], totals[7], totals[8], totals[9], totals[10], totals[11], totals[12], totals[13])
```

```python
import math

import jax
import jax.numpy as jnp
from jax import lax
from jax.sharding import PartitionSpec as P

HD = 64


EPSILON = 1e-06


def layer_norm(hidden, gain, shift):
    center = hidden - jnp.mean(hidden, axis=-1, keepdims=True)
    inverse = lax.rsqrt(jnp.mean(center * center, axis=-1, keepdims=True) + EPSILON)
    normed = center * inverse
    return (normed, inverse, normed * gain + shift)


def norm_back(upstream, normed, inverse, gain):
    scaled = upstream * gain
    return inverse * (
        scaled
        - jnp.mean(scaled, axis=-1, keepdims=True)
        - normed * jnp.mean(scaled * normed, axis=-1, keepdims=True)
    )


def gelu_slope(pre):
    cumulative = 0.5 * (1.0 + jax.scipy.special.erf(pre * 0.7071067811865476))
    return cumulative + pre * jnp.exp(-0.5 * pre * pre) * 0.3989422804014327


def head_view(rows):
    return rows.reshape(rows.shape[0], rows.shape[1], rows.shape[2] // HD, HD)


def masked_scores(queries, key_all, lengths_now):
    scores = jnp.einsum(
        "bqhd,bkhd->bhqk",
        head_view(queries),
        head_view(key_all),
        preferred_element_type=jnp.float32,
    ) * (1.0 / math.sqrt(HD))
    span = key_all.shape[1]
    valid = (
        lax.broadcasted_iota(jnp.int32, (key_all.shape[0], 1, 1, span), 3)
        < lengths_now[:, None, None, None]
    )
    return jnp.where(valid, scores, -jnp.inf)


def attend(queries, key_all, value_all, lengths_now):
    scores = masked_scores(queries, key_all, lengths_now)
    largest = jnp.max(scores, axis=-1, keepdims=True)
    expo = jnp.exp(scores - largest)
    total = jnp.sum(expo, axis=-1, keepdims=True)
    weights = (expo / total).astype(jnp.bfloat16)
    mixed = jnp.einsum(
        "bhqk,bkhd->bqhd", weights, head_view(value_all), preferred_element_type=jnp.float32
    )
    mixed = mixed.reshape(queries.shape).astype(jnp.bfloat16)
    return (mixed, largest + jnp.log(total))


def score_block(query_rows, key_block, value_block, log_total, inner, grad_rows, lengths_now):
    scores = jnp.einsum(
        "bqhd,bkhd->bhqk",
        head_view(query_rows),
        head_view(key_block),
        preferred_element_type=jnp.float32,
    ) * (1.0 / math.sqrt(HD))
    span = key_block.shape[1]
    valid = (
        lax.broadcasted_iota(jnp.int32, (key_block.shape[0], 1, 1, span), 3)
        < lengths_now[:, None, None, None]
    )
    probs = jnp.exp(jnp.where(valid, scores, -jnp.inf) - log_total)
    grad_probs = jnp.einsum(
        "bqhd,bkhd->bhqk",
        head_view(grad_rows),
        head_view(value_block),
        preferred_element_type=jnp.float32,
    )
    grad_scores = (probs * (grad_probs - inner) * (1.0 / math.sqrt(HD))).astype(jnp.bfloat16)
    return (probs.astype(jnp.bfloat16), grad_scores)


def attend_back(queries, key_all, value_all, mixed, log_total, grad_mixed, lengths_now):
    grad_heads = head_view(grad_mixed)
    inner = jnp.sum(grad_heads.astype(jnp.float32) * head_view(mixed).astype(jnp.float32), axis=-1)
    inner = jnp.transpose(inner, (0, 2, 1))[..., None]
    probs_low, grad_scores = score_block(
        queries, key_all, value_all, log_total, inner, grad_mixed, lengths_now
    )
    grad_queries = jnp.einsum(
        "bhqk,bkhd->bqhd", grad_scores, head_view(key_all), preferred_element_type=jnp.float32
    ).reshape(queries.shape)
    grad_keys = jnp.einsum(
        "bhqk,bqhd->bkhd", grad_scores, head_view(queries), preferred_element_type=jnp.float32
    ).reshape(key_all.shape)
    grad_values = jnp.einsum(
        "bhqk,bqhd->bkhd", probs_low, grad_heads, preferred_element_type=jnp.float32
    ).reshape(value_all.shape)
    return (grad_queries, grad_keys, grad_values)


def gather_rows(rows):
    return lax.all_gather(rows, "tensor", axis=1, tiled=True)


def scatter_sum(partial, axis_name):
    devices = lax.axis_size(axis_name)
    shape = partial.shape
    split = partial.reshape(shape[:-2] + (devices, shape[-2] // devices, shape[-1]))
    dim = len(shape) - 2
    moved = lax.all_to_all(split, axis_name, split_axis=dim, concat_axis=dim)
    return jnp.sum(moved.astype(jnp.float32), axis=dim)


def own_rows(rows):
    share = rows.shape[1] // lax.axis_size("tensor")
    return lax.dynamic_slice_in_dim(rows, lax.axis_index("tensor") * share, share, 1)


def pieces_of(rows):
    devices = lax.axis_size("ctx")
    share = rows.shape[-1] // devices
    me = lax.axis_index("ctx")
    return [
        lax.dynamic_slice_in_dim(rows, (me ^ step) * share, share, rows.ndim - 1)
        for step in range(devices)
    ]


def fold_pieces(pieces):
    devices = lax.axis_size("ctx")
    bit = 1
    while len(pieces) > 1:
        pairs = [(i, i ^ bit) for i in range(devices)]
        pieces = [
            keep + lax.ppermute(send.astype(jnp.bfloat16), "ctx", pairs).astype(jnp.float32)
            for keep, send in zip(pieces[0::2], pieces[1::2])
        ]
        bit *= 2
    return pieces[0]


def forward(entry, lengths_now, params):
    hidden, normed_in = entry["hidden"], entry["normed_in"]
    triple = jnp.einsum(
        "bld,kde->kble", normed_in, params["projection"], preferred_element_type=jnp.float32
    )
    queries = (triple[0] + params["query_bias"]).astype(jnp.bfloat16)
    key_rows = triple[1].astype(jnp.bfloat16)
    value_rows = (triple[2] + params["value_bias"]).astype(jnp.bfloat16)
    key_all = lax.all_gather(key_rows, "ctx", axis=1, tiled=True)
    value_all = lax.all_gather(value_rows, "ctx", axis=1, tiled=True)
    mixed, log_total = attend(queries, key_all, value_all, lengths_now)
    merged = scatter_sum(
        jnp.einsum(
            "blc,cd->bld", mixed, params["merger"], preferred_element_type=jnp.float32
        ).astype(jnp.bfloat16),
        "tensor",
    )
    attn_out = merged + params["merger_bias"]
    middle = hidden + params["attention_scale"] * attn_out
    normed_two, inverse_two, pre_two = layer_norm(
        middle, params["second_gain"], params["second_shift"]
    )
    normed_mid = gather_rows(pre_two.astype(jnp.bfloat16))
    expanded = (
        jnp.einsum(
            "bld,df->blf", normed_mid, params["expander"], preferred_element_type=jnp.float32
        )
        + params["expander_bias"]
    )
    activated = jax.nn.gelu(expanded, approximate=False).astype(jnp.bfloat16)
    summed = scatter_sum(
        jnp.einsum(
            "blf,fd->bld", activated, params["reducer"], preferred_element_type=jnp.float32
        ).astype(jnp.bfloat16),
        "tensor",
    )
    reduced = summed + params["reducer_bias"]
    output = middle + params["feedforward_scale"] * reduced
    saved = dict(
        queries=queries,
        key_all=key_all,
        value_all=value_all,
        mixed=mixed,
        log_total=log_total,
        attn_out=attn_out,
        normed_two=normed_two,
        inverse_two=inverse_two,
        normed_mid=normed_mid,
        expanded=expanded,
        activated=activated,
        reduced=reduced,
        **entry,
    )
    return (output, saved)


def row_sum(rows):
    return jnp.sum(rows, axis=(0, 1))


def backward(saved, upstream, reduced_low, lengths_now, params):
    grad_fscale = row_sum(upstream * saved["reduced"])
    grad_rbias = row_sum(upstream * params["feedforward_scale"])
    activated, normed_mid, mixed = saved["activated"], saved["normed_mid"], saved["mixed"]
    grad_act = jnp.einsum(
        "bld,fd->blf", reduced_low, params["reducer"], preferred_element_type=jnp.float32
    )
    grad_pre = grad_act * gelu_slope(saved["expanded"])
    grad_ebias = row_sum(grad_pre)
    pre_low = grad_pre.astype(jnp.bfloat16)
    grad_normed2 = scatter_sum(
        jnp.einsum(
            "blf,df->bld", pre_low, params["expander"], preferred_element_type=jnp.float32
        ).astype(jnp.bfloat16),
        "tensor",
    )
    grad_reducer = fold_pieces(
        [
            jnp.einsum("blf,bld->fd", activated, piece, preferred_element_type=jnp.float32)
            for piece in pieces_of(reduced_low)
        ]
    )
    grad_expander = fold_pieces(
        [
            jnp.einsum("bld,blf->df", piece, pre_low, preferred_element_type=jnp.float32)
            for piece in pieces_of(normed_mid)
        ]
    )
    normed_two = saved["normed_two"]
    grad_sgain = row_sum(grad_normed2 * normed_two)
    grad_sshift = row_sum(grad_normed2)
    grad_middle = upstream + norm_back(
        grad_normed2, normed_two, saved["inverse_two"], params["second_gain"]
    )
    grad_ascale = row_sum(grad_middle * saved["attn_out"])
    grad_attn = grad_middle * params["attention_scale"]
    grad_mbias = row_sum(grad_attn)
    attn_low = gather_rows(grad_attn.astype(jnp.bfloat16))
    grad_mixed = jnp.einsum(
        "bld,cd->blc", attn_low, params["merger"], preferred_element_type=jnp.float32
    ).astype(jnp.bfloat16)
    grad_queries, grad_keys, grad_values = attend_back(
        saved["queries"],
        saved["key_all"],
        saved["value_all"],
        mixed,
        saved["log_total"],
        grad_mixed,
        lengths_now,
    )
    grad_merger = fold_pieces(
        [
            jnp.einsum("blc,bld->cd", mixed, piece, preferred_element_type=jnp.float32)
            for piece in pieces_of(attn_low)
        ]
    )
    key_value = scatter_sum(
        jnp.stack([grad_keys.astype(jnp.bfloat16), grad_values.astype(jnp.bfloat16)]), "ctx"
    )
    grad_qvbias = jnp.stack([row_sum(grad_queries), row_sum(key_value[1])])
    stacked = jnp.concatenate([grad_queries[None], key_value]).astype(jnp.bfloat16)
    grad_normed1 = scatter_sum(
        jnp.einsum(
            "kble,kde->bld", stacked, params["projection"], preferred_element_type=jnp.float32
        ).astype(jnp.bfloat16),
        "tensor",
    )
    grad_projection = fold_pieces(
        [
            jnp.einsum("bld,kble->kde", piece, stacked, preferred_element_type=jnp.float32)
            for piece in pieces_of(saved["normed_in"])
        ]
    )
    normed_one = saved["normed_one"]
    grad_fgain = row_sum(grad_normed1 * normed_one)
    grad_fshift = row_sum(grad_normed1)
    grad_input = grad_middle + norm_back(
        grad_normed1, normed_one, saved["inverse_one"], params["first_gain"]
    )
    weights = (grad_projection, grad_merger, grad_expander, grad_reducer)
    wide = (
        grad_mbias,
        grad_rbias,
        grad_fgain,
        grad_fshift,
        grad_sgain,
        grad_sshift,
        grad_ascale,
        grad_fscale,
    )
    devices = lax.axis_size("ctx")
    vectors = jnp.concatenate(
        [piece.reshape(devices, -1) for piece in wide]
        + [
            grad_ebias.reshape(devices, -1),
            jnp.transpose(grad_qvbias.reshape(2, -1, devices, HD // devices), (2, 0, 1, 3)).reshape(
                devices, -1
            ),
        ],
        axis=1,
    )
    return (grad_input, weights, vectors)


def on_device(
    block_input,
    cotangent,
    lengths,
    projection,
    projectionbias,
    merger,
    mergerbias,
    expander,
    expanderbias,
    reducer,
    reducerbias,
    firstgain,
    firstshift,
    secondgain,
    secondshift,
    attentionscale,
    feedforwardscale,
):
    sections = lax.axis_size("section")
    section = lax.axis_index("section")
    ctx = lax.axis_size("ctx")
    micro, images, rows, width = block_input.shape
    per_section = micro // sections
    share = width // ctx

    def own_images(array):
        return lax.dynamic_slice_in_dim(array, section * per_section, per_section, 0)

    own_input = own_images(block_input).reshape(per_section * images, rows, width)
    own_input = own_input.astype(jnp.float32)
    own_cotangent = own_images(cotangent).reshape(per_section * images, rows, width)
    own_cotangent = own_cotangent.astype(jnp.float32)
    own_lengths = own_images(lengths).reshape(-1)

    packed = jnp.concatenate(
        [
            piece.reshape(-1)
            for piece in (
                mergerbias,
                reducerbias,
                firstgain,
                firstshift,
                secondgain,
                secondshift,
                attentionscale,
                feedforwardscale,
                expanderbias,
                projectionbias,
            )
        ]
    )
    packed_all = lax.all_gather(packed, ("section", "ctx")).astype(jnp.float32)
    packed_all = packed_all.reshape(sections, ctx, -1)
    hidden_share = expanderbias.shape[-1]
    names = (
        "merger_bias",
        "reducer_bias",
        "first_gain",
        "first_shift",
        "second_gain",
        "second_shift",
        "attention_scale",
        "feedforward_scale",
    )

    def layer_params(layer):
        params = {}
        for key, shard, axis in (
            ("projection", projection, 1),
            ("merger", merger, 1),
            ("expander", expander, 0),
            ("reducer", reducer, 1),
        ):
            sent = lax.ppermute(
                shard[0], "section", [(layer, other) for other in range(sections) if other != layer]
            )
            held = jnp.where(section == layer, shard[0], sent)
            params[key] = lax.all_gather(held, "ctx", axis=axis, tiled=True)
        flat = packed_all[layer]
        for number, name in enumerate(names):
            params[name] = flat[:, number * share : (number + 1) * share].reshape(-1)
        start = len(names) * share
        params["expander_bias"] = flat[:, start : start + hidden_share].reshape(-1)
        start += hidden_share
        bias = flat[:, start:].reshape(ctx, 2, -1, HD // ctx)
        bias = jnp.transpose(bias, (1, 2, 0, 3)).reshape(2, -1)
        params["query_bias"], params["value_bias"] = bias[0], bias[1]
        return params

    layers = [layer_params(layer) for layer in range(sections)]

    stash = []
    for layer, params in enumerate(layers):
        gain, shift = params["first_gain"], params["first_shift"]
        if layer == 0:
            hidden = own_rows(own_input)
            normed_in = layer_norm(own_input, gain, shift)[2].astype(jnp.bfloat16)
            normed_one, inverse_one, _ = layer_norm(hidden, gain, shift)
        else:
            hidden = leaving.astype(jnp.bfloat16).astype(jnp.float32)
            normed_one, inverse_one, pre_one = layer_norm(hidden, gain, shift)
            normed_in = gather_rows(pre_one.astype(jnp.bfloat16))
        entry = dict(
            hidden=hidden, normed_in=normed_in, normed_one=normed_one, inverse_one=inverse_one
        )
        leaving, saved = forward(entry, own_lengths, params)
        stash.append(saved)

    upstream = own_rows(own_cotangent)
    weight_terms, vector_terms = [None] * sections, [None] * sections
    for layer in reversed(range(sections)):
        params = layers[layer]
        if layer == sections - 1:
            reduced_low = (own_cotangent * params["feedforward_scale"]).astype(jnp.bfloat16)
        else:
            reduced_low = gather_rows((upstream * params["feedforward_scale"]).astype(jnp.bfloat16))
        upstream, weights, vectors = backward(
            stash[layer], upstream, reduced_low, own_lengths, params
        )
        arrived = []
        for grad in weights:
            low = grad.astype(jnp.bfloat16)
            total = grad
            for step in range(1, sections):
                source = (layer + step) % sections
                total = total + lax.ppermute(low, "section", [(source, layer)]).astype(jnp.float32)
            arrived.append(total)
        weight_terms[layer], vector_terms[layer] = arrived, vectors

    grads = []
    for number in range(4):
        chosen = weight_terms[0][number]
        for layer in range(1, sections):
            chosen = jnp.where(section == layer, weight_terms[layer][number], chosen)
        grads.append(chosen[None])

    vectors = jnp.stack(vector_terms, axis=1)
    vectors = jnp.sum(lax.all_to_all(vectors, "ctx", split_axis=0, concat_axis=0), axis=0)
    tensor = lax.axis_size("tensor")
    spread = lax.all_gather(vectors, ("section", "tensor")).reshape(
        sections, tensor, sections, -1
    )
    spread = jnp.sum(spread, axis=0)
    spread = lax.dynamic_index_in_dim(spread, section, 1, keepdims=False)
    wide = len(names) * share
    summed = jnp.sum(spread[:, :wide], axis=0).reshape(len(names), 1, share)
    mine = lax.dynamic_index_in_dim(spread[:, wide:], lax.axis_index("tensor"), 0, keepdims=False)
    grad_ebias = mine[:hidden_share].reshape(expanderbias.shape)
    grad_qvbias = mine[hidden_share:].reshape(projectionbias.shape)

    def place(own):
        parts = own.astype(jnp.bfloat16).reshape(own.shape[0], own.shape[1], sections, -1)
        parts = jnp.moveaxis(parts, 2, 0)
        parts = lax.all_to_all(parts, "section", split_axis=0, concat_axis=0)
        parts = parts.reshape((micro * images,) + parts.shape[2:])
        return gather_rows(parts).reshape(micro, images, rows, -1)

    block_output = place(leaving)
    input_grad = place(upstream).astype(jnp.float32)
    return (
        block_output,
        input_grad,
        grads[0],
        grad_qvbias,
        grads[1],
        summed[0],
        grads[2],
        grad_ebias,
        grads[3],
        summed[1],
        summed[2],
        summed[3],
        summed[4],
        summed[5],
        summed[6],
        summed[7],
    )


def solution(mesh):
    in_specs = (
        P(None, None, "ctx", None),
        P(None, None, "ctx", None),
        P(),
        P("section", None, "ctx", "tensor"),
        P("section", None, "tensor", "ctx"),
        P("section", "tensor", "ctx"),
        P("section", "ctx"),
        P("section", "ctx", "tensor"),
        P("section", "tensor", "ctx"),
        P("section", "tensor", "ctx"),
        P("section", "ctx"),
        P("section", "ctx"),
        P("section", "ctx"),
        P("section", "ctx"),
        P("section", "ctx"),
        P("section", "ctx"),
        P("section", "ctx"),
    )
    out_specs = (
        P(None, None, "ctx", "section"),
        P(None, None, "ctx", "section"),
        P("section", None, "ctx", "tensor"),
        P("section", None, "tensor", "ctx"),
        P("section", "tensor", "ctx"),
        P("section", "ctx"),
        P("section", "ctx", "tensor"),
        P("section", "tensor", "ctx"),
        P("section", "tensor", "ctx"),
        P("section", "ctx"),
        P("section", "ctx"),
        P("section", "ctx"),
        P("section", "ctx"),
        P("section", "ctx"),
        P("section", "ctx"),
        P("section", "ctx"),
    )
    return jax.shard_map(
        on_device, mesh=mesh, in_specs=in_specs, out_specs=out_specs, check_vma=False
    )
```

```python
import math
from types import SimpleNamespace

import jax
import jax.numpy as jnp
from jax import lax
from jax.sharding import PartitionSpec as P

HD = 64
SECTION, CTX, TENSOR = "section", "ctx", "tensor"


EPSILON = 1e-06


def layer_norm(hidden, gain, shift):
    center = hidden - jnp.mean(hidden, axis=-1, keepdims=True)
    inverse = lax.rsqrt(jnp.mean(center * center, axis=-1, keepdims=True) + EPSILON)
    normed = center * inverse
    return (normed, inverse, normed * gain + shift)


def norm_back(upstream, normed, inverse, gain):
    scaled = upstream * gain
    return inverse * (
        scaled
        - jnp.mean(scaled, axis=-1, keepdims=True)
        - normed * jnp.mean(scaled * normed, axis=-1, keepdims=True)
    )


def gelu_slope(pre):
    cumulative = 0.5 * (1.0 + jax.scipy.special.erf(pre * 0.7071067811865476))
    return cumulative + pre * jnp.exp(-0.5 * pre * pre) * 0.3989422804014327


def head_view(rows):
    return rows.reshape(rows.shape[0], rows.shape[1], rows.shape[2] // HD, HD)


def masked_scores(queries, key_all, lengths_now):
    scores = jnp.einsum(
        "bqhd,bkhd->bhqk",
        head_view(queries),
        head_view(key_all),
        preferred_element_type=jnp.float32,
    ) * (1.0 / math.sqrt(HD))
    span = key_all.shape[1]
    valid = (
        lax.broadcasted_iota(jnp.int32, (key_all.shape[0], 1, 1, span), 3)
        < lengths_now[:, None, None, None]
    )
    return jnp.where(valid, scores, -jnp.inf)


def attend(queries, key_all, value_all, lengths_now):
    scores = masked_scores(queries, key_all, lengths_now)
    largest = jnp.max(scores, axis=-1, keepdims=True)
    expo = jnp.exp(scores - largest)
    total = jnp.sum(expo, axis=-1, keepdims=True)
    weights = (expo / total).astype(jnp.bfloat16)
    mixed = jnp.einsum(
        "bhqk,bkhd->bqhd", weights, head_view(value_all), preferred_element_type=jnp.float32
    )
    mixed = mixed.reshape(queries.shape).astype(jnp.bfloat16)
    return (mixed, largest + jnp.log(total))


def score_block(query_rows, key_block, value_block, log_total, inner, grad_rows, lengths_now):
    scores = jnp.einsum(
        "bqhd,bkhd->bhqk",
        head_view(query_rows),
        head_view(key_block),
        preferred_element_type=jnp.float32,
    ) * (1.0 / math.sqrt(HD))
    span = key_block.shape[1]
    valid = (
        lax.broadcasted_iota(jnp.int32, (key_block.shape[0], 1, 1, span), 3)
        < lengths_now[:, None, None, None]
    )
    probs = jnp.exp(jnp.where(valid, scores, -jnp.inf) - log_total)
    grad_probs = jnp.einsum(
        "bqhd,bkhd->bhqk",
        head_view(grad_rows),
        head_view(value_block),
        preferred_element_type=jnp.float32,
    )
    grad_scores = (probs * (grad_probs - inner) * (1.0 / math.sqrt(HD))).astype(jnp.bfloat16)
    return (probs.astype(jnp.bfloat16), grad_scores)


def attend_back(queries, key_all, value_all, mixed, log_total, grad_mixed, lengths_now):
    grad_heads = head_view(grad_mixed)
    inner = jnp.sum(grad_heads.astype(jnp.float32) * head_view(mixed).astype(jnp.float32), axis=-1)
    inner = jnp.transpose(inner, (0, 2, 1))[..., None]
    probs_low, grad_scores = score_block(
        queries, key_all, value_all, log_total, inner, grad_mixed, lengths_now
    )
    grad_queries = jnp.einsum(
        "bhqk,bkhd->bqhd", grad_scores, head_view(key_all), preferred_element_type=jnp.float32
    ).reshape(queries.shape)
    grad_keys = jnp.einsum(
        "bhqk,bqhd->bkhd", grad_scores, head_view(queries), preferred_element_type=jnp.float32
    ).reshape(key_all.shape)
    grad_values = jnp.einsum(
        "bhqk,bqhd->bkhd", probs_low, grad_heads, preferred_element_type=jnp.float32
    ).reshape(value_all.shape)
    return (grad_queries, grad_keys, grad_values)


def gather_rows(rows):
    return lax.all_gather(rows, TENSOR, axis=1, tiled=True)


def scatter_sum(partial, axis_name):
    devices = lax.axis_size(axis_name)
    shape = partial.shape
    split = partial.reshape(shape[:-2] + (devices, shape[-2] // devices, shape[-1]))
    dim = len(shape) - 2
    moved = lax.all_to_all(split, axis_name, split_axis=dim, concat_axis=dim)
    return jnp.sum(moved.astype(jnp.float32), axis=dim)


def own_rows(rows):
    share = rows.shape[1] // lax.axis_size(TENSOR)
    return lax.dynamic_slice_in_dim(rows, lax.axis_index(TENSOR) * share, share, 1)


def pieces_of(rows):
    devices = lax.axis_size(CTX)
    share = rows.shape[-1] // devices
    me = lax.axis_index(CTX)
    return [
        lax.dynamic_slice_in_dim(rows, (me ^ step) * share, share, rows.ndim - 1)
        for step in range(devices)
    ]


def fold_pieces(pieces):
    devices = lax.axis_size(CTX)
    bit = 1
    while len(pieces) > 1:
        pairs = [(i, i ^ bit) for i in range(devices)]
        pieces = [
            keep + lax.ppermute(send.astype(jnp.bfloat16), CTX, pairs).astype(jnp.float32)
            for keep, send in zip(pieces[0::2], pieces[1::2])
        ]
        bit *= 2
    return pieces[0]


def forward(entry, lengths_now, params):
    hidden, normed_in = entry.hidden, entry.normed_in
    triple = jnp.einsum(
        "bld,kde->kble", normed_in, params.projection, preferred_element_type=jnp.float32
    )
    queries = (triple[0] + params.query_bias).astype(jnp.bfloat16)
    key_rows = triple[1].astype(jnp.bfloat16)
    value_rows = (triple[2] + params.value_bias).astype(jnp.bfloat16)
    key_all = lax.all_gather(key_rows, CTX, axis=1, tiled=True)
    value_all = lax.all_gather(value_rows, CTX, axis=1, tiled=True)
    mixed, log_total = attend(queries, key_all, value_all, lengths_now)
    merged = scatter_sum(
        jnp.einsum(
            "blc,cd->bld", mixed, params.merger, preferred_element_type=jnp.float32
        ).astype(jnp.bfloat16),
        TENSOR,
    )
    attn_out = merged + params.merger_bias
    middle = hidden + params.attention_scale * attn_out
    normed_two, inverse_two, pre_two = layer_norm(
        middle, params.second_gain, params.second_shift
    )
    normed_mid = gather_rows(pre_two.astype(jnp.bfloat16))
    expanded = (
        jnp.einsum(
            "bld,df->blf", normed_mid, params.expander, preferred_element_type=jnp.float32
        )
        + params.expander_bias
    )
    activated = jax.nn.gelu(expanded, approximate=False).astype(jnp.bfloat16)
    summed = scatter_sum(
        jnp.einsum(
            "blf,fd->bld", activated, params.reducer, preferred_element_type=jnp.float32
        ).astype(jnp.bfloat16),
        TENSOR,
    )
    reduced = summed + params.reducer_bias
    output = middle + params.feedforward_scale * reduced
    saved = SimpleNamespace(
        queries=queries,
        key_all=key_all,
        value_all=value_all,
        mixed=mixed,
        log_total=log_total,
        attn_out=attn_out,
        normed_two=normed_two,
        inverse_two=inverse_two,
        normed_mid=normed_mid,
        expanded=expanded,
        activated=activated,
        reduced=reduced,
        normed_in=normed_in,
        normed_one=entry.normed_one,
        inverse_one=entry.inverse_one,
    )
    return (output, saved)


def row_sum(rows):
    return jnp.sum(rows, axis=(0, 1))


def backward(saved, upstream, reduced_low, lengths_now, params):
    grad_fscale = row_sum(upstream * saved.reduced)
    grad_rbias = row_sum(upstream * params.feedforward_scale)
    activated, normed_mid, mixed = saved.activated, saved.normed_mid, saved.mixed
    grad_act = jnp.einsum(
        "bld,fd->blf", reduced_low, params.reducer, preferred_element_type=jnp.float32
    )
    grad_pre = grad_act * gelu_slope(saved.expanded)
    grad_ebias = row_sum(grad_pre)
    pre_low = grad_pre.astype(jnp.bfloat16)
    grad_normed2 = scatter_sum(
        jnp.einsum(
            "blf,df->bld", pre_low, params.expander, preferred_element_type=jnp.float32
        ).astype(jnp.bfloat16),
        TENSOR,
    )
    grad_reducer = fold_pieces(
        [
            jnp.einsum("blf,bld->fd", activated, piece, preferred_element_type=jnp.float32)
            for piece in pieces_of(reduced_low)
        ]
    )
    grad_expander = fold_pieces(
        [
            jnp.einsum("bld,blf->df", piece, pre_low, preferred_element_type=jnp.float32)
            for piece in pieces_of(normed_mid)
        ]
    )
    normed_two = saved.normed_two
    grad_sgain = row_sum(grad_normed2 * normed_two)
    grad_sshift = row_sum(grad_normed2)
    grad_middle = upstream + norm_back(
        grad_normed2, normed_two, saved.inverse_two, params.second_gain
    )
    grad_ascale = row_sum(grad_middle * saved.attn_out)
    grad_attn = grad_middle * params.attention_scale
    grad_mbias = row_sum(grad_attn)
    attn_low = gather_rows(grad_attn.astype(jnp.bfloat16))
    grad_mixed = jnp.einsum(
        "bld,cd->blc", attn_low, params.merger, preferred_element_type=jnp.float32
    ).astype(jnp.bfloat16)
    grad_queries, grad_keys, grad_values = attend_back(
        saved.queries,
        saved.key_all,
        saved.value_all,
        mixed,
        saved.log_total,
        grad_mixed,
        lengths_now,
    )
    grad_merger = fold_pieces(
        [
            jnp.einsum("blc,bld->cd", mixed, piece, preferred_element_type=jnp.float32)
            for piece in pieces_of(attn_low)
        ]
    )
    key_value = scatter_sum(
        jnp.stack([grad_keys.astype(jnp.bfloat16), grad_values.astype(jnp.bfloat16)]), CTX
    )
    grad_qvbias = jnp.stack([row_sum(grad_queries), row_sum(key_value[1])])
    stacked = jnp.concatenate([grad_queries[None], key_value]).astype(jnp.bfloat16)
    grad_normed1 = scatter_sum(
        jnp.einsum(
            "kble,kde->bld", stacked, params.projection, preferred_element_type=jnp.float32
        ).astype(jnp.bfloat16),
        TENSOR,
    )
    grad_projection = fold_pieces(
        [
            jnp.einsum("bld,kble->kde", piece, stacked, preferred_element_type=jnp.float32)
            for piece in pieces_of(saved.normed_in)
        ]
    )
    normed_one = saved.normed_one
    grad_fgain = row_sum(grad_normed1 * normed_one)
    grad_fshift = row_sum(grad_normed1)
    grad_input = grad_middle + norm_back(
        grad_normed1, normed_one, saved.inverse_one, params.first_gain
    )
    weights = (grad_projection, grad_merger, grad_expander, grad_reducer)
    wide = (
        grad_mbias,
        grad_rbias,
        grad_fgain,
        grad_fshift,
        grad_sgain,
        grad_sshift,
        grad_ascale,
        grad_fscale,
    )
    devices = lax.axis_size(CTX)
    vectors = jnp.concatenate(
        [piece.reshape(devices, -1) for piece in wide]
        + [
            grad_ebias.reshape(devices, -1),
            jnp.transpose(grad_qvbias.reshape(2, -1, devices, HD // devices), (2, 0, 1, 3)).reshape(
                devices, -1
            ),
        ],
        axis=1,
    )
    return (grad_input, weights, vectors)


def on_device(
    block_input,
    cotangent,
    lengths,
    projection,
    projectionbias,
    merger,
    mergerbias,
    expander,
    expanderbias,
    reducer,
    reducerbias,
    firstgain,
    firstshift,
    secondgain,
    secondshift,
    attentionscale,
    feedforwardscale,
):
    sections = lax.axis_size(SECTION)
    section = lax.axis_index(SECTION)
    ctx = lax.axis_size(CTX)
    micro, images, rows, width = block_input.shape
    per_section = micro // sections
    share = width // ctx

    def own_images(array):
        return lax.dynamic_slice_in_dim(array, section * per_section, per_section, 0)

    own_input = own_images(block_input).reshape(per_section * images, rows, width)
    own_input = own_input.astype(jnp.float32)
    own_cotangent = own_images(cotangent).reshape(per_section * images, rows, width)
    own_cotangent = own_cotangent.astype(jnp.float32)
    own_lengths = own_images(lengths).reshape(-1)

    hidden_share = expanderbias.shape[-1]
    wide_vectors = (
        mergerbias,
        reducerbias,
        firstgain,
        firstshift,
        secondgain,
        secondshift,
        attentionscale,
        feedforwardscale,
    )

    def as_rows(vector):
        flat = vector.reshape(-1)
        return jnp.pad(flat, (0, -flat.size % share)).reshape(-1, share)

    packed = jnp.concatenate([as_rows(v) for v in wide_vectors + (expanderbias, projectionbias)])
    packed_all = lax.all_gather(packed, (SECTION, CTX))
    packed_all = packed_all.reshape((sections, ctx) + packed.shape)
    packed_all = jnp.transpose(packed_all, (0, 2, 1, 3)).astype(jnp.float32)
    count = len(wide_vectors)
    hidden_rows = -(-hidden_share // share)

    swapped = [
        lax.ppermute(shard[0], SECTION, [(i, sections - 1 - i) for i in range(sections)])
        for shard in (projection, merger, expander, reducer)
    ]

    def layer_params(layer):
        params = SimpleNamespace()
        held = [
            jnp.where(section == layer, shard[0], other)
            for shard, other in zip((projection, merger, expander, reducer), swapped)
        ]
        params.projection, params.merger, params.expander, params.reducer = (
            lax.all_gather(shard, CTX, axis=axis, tiled=True)
            for shard, axis in zip(held, (1, 1, 0, 1))
        )
        table = packed_all[layer]
        (
            params.merger_bias,
            params.reducer_bias,
            params.first_gain,
            params.first_shift,
            params.second_gain,
            params.second_shift,
            params.attention_scale,
            params.feedforward_scale,
        ) = (table[number].reshape(-1) for number in range(count))
        hidden = jnp.swapaxes(table[count : count + hidden_rows], 0, 1).reshape(ctx, -1)
        params.expander_bias = hidden[:, :hidden_share].reshape(-1)
        bias = jnp.swapaxes(table[count + hidden_rows :], 0, 1).reshape(ctx, -1)
        bias = bias[:, : projectionbias.size].reshape(ctx, 2, -1, HD // ctx)
        bias = jnp.transpose(bias, (1, 2, 0, 3)).reshape(2, -1)
        params.query_bias, params.value_bias = bias[0], bias[1]
        return params

    layers = [layer_params(layer) for layer in range(sections)]

    stash = []
    for layer, params in enumerate(layers):
        gain, shift = params.first_gain, params.first_shift
        if layer == 0:
            hidden = own_rows(own_input)
            normed_in = layer_norm(own_input, gain, shift)[2].astype(jnp.bfloat16)
            normed_one, inverse_one, _ = layer_norm(hidden, gain, shift)
        else:
            hidden = leaving.astype(jnp.bfloat16).astype(jnp.float32)
            normed_one, inverse_one, pre_one = layer_norm(hidden, gain, shift)
            normed_in = gather_rows(pre_one.astype(jnp.bfloat16))
        entry = SimpleNamespace(
            hidden=hidden, normed_in=normed_in, normed_one=normed_one, inverse_one=inverse_one
        )
        leaving, saved = forward(entry, own_lengths, params)
        stash.append(saved)

    upstream = own_rows(own_cotangent)
    weight_terms, vector_terms = [None] * sections, [None] * sections
    for layer in reversed(range(sections)):
        params = layers[layer]
        if layer == sections - 1:
            reduced_low = (own_cotangent * params.feedforward_scale).astype(jnp.bfloat16)
        else:
            reduced_low = gather_rows((upstream * params.feedforward_scale).astype(jnp.bfloat16))
        upstream, weights, vectors = backward(
            stash[layer], upstream, reduced_low, own_lengths, params
        )
        arrived = []
        for grad in weights:
            low = grad.astype(jnp.bfloat16)
            total = grad
            for step in range(1, sections):
                source = (layer + step) % sections
                total = total + lax.ppermute(low, SECTION, [(source, layer)]).astype(jnp.float32)
            arrived.append(total)
        weight_terms[layer], vector_terms[layer] = arrived, vectors

    grads = []
    for number in range(4):
        chosen = weight_terms[0][number]
        for layer in range(1, sections):
            chosen = jnp.where(section == layer, weight_terms[layer][number], chosen)
        grads.append(chosen[None])

    vectors = jnp.stack(vector_terms)
    vectors = vectors.reshape((sections * ctx,) + vectors.shape[2:])
    vectors = lax.all_to_all(vectors, (SECTION, CTX), split_axis=0, concat_axis=0)
    vectors = jnp.sum(vectors, axis=0)
    wide = count * share
    spread = lax.all_gather(vectors[:wide], TENSOR)
    summed = jnp.sum(spread, axis=0).reshape(count, 1, share)
    mine = vectors[wide:]
    grad_ebias = mine[:hidden_share].reshape(expanderbias.shape)
    grad_qvbias = mine[hidden_share:].reshape(projectionbias.shape)

    tensor = lax.axis_size(TENSOR)

    def place(own):
        parts = own.astype(jnp.bfloat16).reshape(own.shape[0], own.shape[1], sections, -1)
        parts = jnp.moveaxis(parts, 2, 0)[:, None]
        parts = jnp.broadcast_to(parts, (sections, tensor) + parts.shape[2:])
        parts = parts.reshape((sections * tensor,) + parts.shape[2:])
        parts = lax.all_to_all(parts, (SECTION, TENSOR), split_axis=0, concat_axis=0)
        parts = parts.reshape((sections, tensor) + parts.shape[1:])
        return jnp.moveaxis(parts, 1, 2).reshape(micro, images, rows, -1)

    block_output = place(leaving)
    input_grad = place(upstream).astype(jnp.float32)
    return (
        block_output,
        input_grad,
        grads[0],
        grad_qvbias,
        grads[1],
        summed[0],
        grads[2],
        grad_ebias,
        grads[3],
        summed[1],
        summed[2],
        summed[3],
        summed[4],
        summed[5],
        summed[6],
        summed[7],
    )


def solution(mesh):
    in_specs = (
        P(None, None, CTX, None),
        P(None, None, CTX, None),
        P(),
        P(SECTION, None, CTX, TENSOR),
        P(SECTION, None, TENSOR, CTX),
        P(SECTION, TENSOR, CTX),
        P(SECTION, CTX),
        P(SECTION, CTX, TENSOR),
        P(SECTION, TENSOR, CTX),
        P(SECTION, TENSOR, CTX),
        P(SECTION, CTX),
        P(SECTION, CTX),
        P(SECTION, CTX),
        P(SECTION, CTX),
        P(SECTION, CTX),
        P(SECTION, CTX),
        P(SECTION, CTX),
    )
    out_specs = (
        P(None, None, CTX, SECTION),
        P(None, None, CTX, SECTION),
        P(SECTION, None, CTX, TENSOR),
        P(SECTION, None, TENSOR, CTX),
        P(SECTION, TENSOR, CTX),
        P(SECTION, CTX),
        P(SECTION, CTX, TENSOR),
        P(SECTION, TENSOR, CTX),
        P(SECTION, TENSOR, CTX),
        P(SECTION, CTX),
        P(SECTION, CTX),
        P(SECTION, CTX),
        P(SECTION, CTX),
        P(SECTION, CTX),
        P(SECTION, CTX),
        P(SECTION, CTX),
    )
    return jax.shard_map(
        on_device, mesh=mesh, in_specs=in_specs, out_specs=out_specs, check_vma=False
    )
```
